32 devices in a mesh: param: 2 (over x), feat: 4 (over z), ex: 4 (over y, core).
Axes of the slice: x: 2, y: 2, z: 4, core: 2. Of those that a mesh axis runs over, the one named last changes fastest.
Arguments:
- gradients: float32 [2048, 2048], P('ex', 'param'), may hold values from -6 to 6
- projection: float32 [2048, 16, 4, 256], P('param', None, 'feat'), may hold values from -0.125 to 0.125
- factor: float32 [16, 4, 256, 1024], P(None, 'feat', 'param'), may hold values from -0.1875 to 0.1875
- diag_inverse: float32 [4, 256, 256], P(None, 'param'), may hold values from -1 to 1.5, as said below
- queries: float32 [16, 4, 256, 256], P(None, 'feat', 'param', 'ex'), may hold values from -6 to 6
Outputs:
- scores: float32 [256, 2048], P('param', 'ex')
- trailing: float32 [16, 4, 256, 2048], P(None, 'feat', 'param', 'ex')
- trailing_queries: float32 [16, 4, 256, 256], P(None, 'feat', 'param', 'ex')
The draws below stay inside these ranges and needn't reach their ends.
Inputs may be any that keep to these rules, and one draw needn't show every extreme that they name: `diag_inverse`: every block is upper triangular, with diagonal entries of 0.5 to 1.5.
All inputs are finite; a program needn't handle non-finite values.
Results may differ from the reference program's by a relative error of at most 0.00017.
Values sent between devices are 32-bit elements; how exact they have to be, the bound alone decides.
No kernel may reach another device: no remote copies, remote signals or barrier semaphores. Data moves between devices by JAX's collectives and lax.ppermute only.
A program may use at most 128 MiB of HBM per device.

```python
import math
import jax
import jax.numpy as jnp
from jax import lax

PANEL = 256
SOLVED = 4
ROUNDS = 16
W = 1024
NEX = 2048
NQ = 256
P_SIZE = 2048
N_FEAT = 4


def draw_diag_inverse(key, part):
    first_key, second_key = jax.random.split(jax.random.fold_in(key, 17))
    indices = jnp.arange(PANEL)
    above = (indices[None, :] > indices[:, None]).astype(jnp.float32)
    spread = jax.random.normal(first_key, (SOLVED, PANEL, PANEL), jnp.float32)
    diagonal = jnp.exp(jax.random.uniform(second_key, (SOLVED, PANEL), jnp.float32, jnp.log(0.5), jnp.log(1.5)))
    identity = (indices[None, :] == indices[:, None]).astype(jnp.float32)
    return spread * above * (0.7 / jnp.sqrt(PANEL * 1.0)) + diagonal[:, :, None] * identity[None]


def shard_levels(own_key, shape, shards, low, largest):
    factor_of, own = 1.0, jax.random.fold_in(own_key, 6)
    for axis_at, parts in shards:
        steps = jnp.exp(jax.random.uniform(jax.random.fold_in(own, axis_at), (parts,), jnp.float32, low / len(shards), largest / len(shards)))
        factor_of = factor_of * jnp.repeat(steps, shape[axis_at] // parts).reshape([-1 if axis == axis_at else 1 for axis in range(len(shape))])
    return factor_of


def bell_draw(key, extent, width, most, cuts=(), held_as=jnp.bfloat16):
    loudness = shard_levels(key, extent, cuts, -0.22, 0.18) if cuts else 1.0
    array = jax.random.normal(key, extent, jnp.float32) * width * loudness
    return jnp.minimum(jnp.maximum(array, -most), most).astype(held_as)


def setup_inputs(seed: int = 0) -> dict:
    key_of = jax.random.split(jax.random.key(seed), 6)
    gradients = bell_draw(key_of[0], (NEX, P_SIZE), 1.0, 6.0, ((0, 4), (1, 2)), jnp.float32)
    projection = bell_draw(key_of[1], (P_SIZE, ROUNDS, N_FEAT, PANEL), P_SIZE ** -0.5, 0.125, ((0, 2), (2, 4)), jnp.float32)
    factor = bell_draw(key_of[2], (ROUNDS, N_FEAT, PANEL, W), W ** -0.5, 0.1875, ((1, 4), (2, 2)), jnp.float32)
    diag_inverse = draw_diag_inverse(jax.random.fold_in(key_of[5], 71), 0)
    queries = bell_draw(key_of[4], (ROUNDS, N_FEAT, PANEL, NQ), 1.0, 6.0, ((1, 4), (2, 2), (3, 4)), jnp.float32)
    return dict(gradients=gradients, projection=projection, factor=factor, diag_inverse=diag_inverse, queries=queries)


exact_mode = lax.Precision.HIGHEST

def reference(gradients, projection, factor, diag_inverse, queries):
    projected = jnp.einsum('ep,pmdr->mdre', gradients, projection, precision=exact_mode)
    right_sides = jnp.concatenate([projected, queries], axis=3)
    panel_order = jnp.arange(ROUNDS)[:, None] * N_FEAT + jnp.arange(N_FEAT)[None, :]
    solved_list = []
    for panel_index in range(SOLVED):
        round_index = panel_index // N_FEAT
        owner_index = panel_index % N_FEAT
        solved = jnp.einsum('kr,kc->rc', diag_inverse[panel_index], right_sides[round_index, owner_index], precision=exact_mode)
        columns = factor[:, :, :, panel_index * PANEL:(panel_index + 1) * PANEL]
        update = jnp.einsum('mdrk,kc->mdrc', columns, solved, precision=exact_mode)
        right_sides = jnp.where((panel_order > panel_index)[:, :, None, None], right_sides - update, right_sides)
        solved_list.append(solved)
    window = jnp.concatenate(solved_list, axis=0)
    scores = jnp.einsum('kq,ke->qe', window[:, NEX:], window[:, :NEX], precision=exact_mode) / math.sqrt(W)
    return (scores, right_sides[..., :NEX], right_sides[..., NEX:])
```

```python
import functools
import math

import jax
import jax.numpy as jnp
from jax import lax
from jax.experimental import pallas as pl
from jax.experimental.pallas import tpu as pltpu
from jax.sharding import PartitionSpec as P

exact_mode = lax.Precision.HIGHEST
NN = (((1,), (0,)), ((), ()))
NT = (((1,), (1,)), ((), ()))
SMEM_SPEC = pl.BlockSpec(memory_space=pltpu.SMEM)
ANY_SPEC = pl.BlockSpec(memory_space=pl.ANY)


def broadcast(block, axis, holder):
    block = jnp.where(lax.axis_index(axis) == holder, block, jnp.zeros_like(block))
    return lax.psum(block, axis)


def plain_device(gradients, projection, factor, diag_inverse, queries):
    feat_count = lax.axis_size("feat")
    param_count = lax.axis_size("param")
    rounds = projection.shape[1]
    panel_size = projection.shape[3]
    ex_rows = gradients.shape[0]
    panel_total = diag_inverse.shape[0]
    weights = projection[:, :, 0, :]
    projected = lax.psum_scatter(
        jnp.einsum("ep,pmr->rme", gradients, weights, precision=exact_mode),
        "param",
        scatter_dimension=0,
        tiled=True,
    )
    right_sides = jnp.concatenate([jnp.transpose(projected, (1, 0, 2)), queries[:, 0]], axis=2)
    factor_rows = factor[:, 0]
    feat_place = lax.axis_index("feat")
    panel_order = jnp.arange(rounds) * feat_count + feat_place
    solved_list = []
    for panel_index in range(panel_total):
        root_index = panel_index % feat_count
        panel_rows = right_sides[panel_index // feat_count]
        inverse_rows = diag_inverse[panel_index]
        spread_rows = broadcast(panel_rows, "feat", root_index)
        solved = jnp.einsum(
            "kr,kc->rc",
            lax.all_gather(inverse_rows, "param", axis=0, tiled=True),
            lax.all_gather(spread_rows, "param", axis=0, tiled=True),
            precision=exact_mode,
        )
        apply_columns = factor_rows[:, :, panel_index * panel_size : (panel_index + 1) * panel_size]
        update = jnp.einsum("mrk,kc->mrc", apply_columns, solved, precision=exact_mode)
        right_sides = jnp.where(
            (panel_order > panel_index)[:, None, None], right_sides - update, right_sides
        )
        solved_list.append(solved)
    window = jnp.concatenate(solved_list, axis=0)
    train_part = window[:, :ex_rows]
    query_part = lax.all_gather(window[:, ex_rows:], "ex", axis=1, tiled=True)
    slice_width = query_part.shape[1] // param_count
    own_queries = lax.dynamic_slice_in_dim(
        query_part, lax.axis_index("param") * slice_width, slice_width, 1
    )
    scores = jnp.einsum("kq,ke->qe", own_queries, train_part, precision=exact_mode) / math.sqrt(
        window.shape[0]
    )
    trailing = right_sides[:, None, :, :ex_rows]
    trailing_queries = right_sides[:, None, :, ex_rows:]
    return (scores, trailing, trailing_queries)


def split(value):
    high = value.astype(jnp.bfloat16)
    low = (value - high.astype(jnp.float32)).astype(jnp.bfloat16)
    return high, low


def product(left, right, dims):
    left_high, left_low = left
    right_high, right_low = right
    dot = functools.partial(lax.dot_general, dimension_numbers=dims, preferred_element_type=jnp.float32)
    return dot(left_high, right_high) + (dot(left_high, right_low) + dot(left_low, right_high))


def project_first_kernel(place, g_ref, p_ref, q_ref, own_ref, send_ref, part_ref):
    ex_rows = g_ref.shape[0]
    half = p_ref.shape[2]
    first = place[0] == 0
    grads = split(g_ref[...])
    for i in range(own_ref.shape[0]):
        weights = jnp.concatenate([p_ref[:, 2 * i, :], p_ref[:, 2 * i + 1, :]], axis=1)
        out = product(grads, split(weights), NN)
        own_ref[i] = jnp.where(first, out[:, :half], out[:, half:])
        if i == 0:
            part_ref[:ex_rows, :] = out
            rows = q_ref[0]
            zero = jnp.zeros_like(rows)
            part_ref[ex_rows:, :half] = jnp.where(first, rows, zero)
            part_ref[ex_rows:, half:] = jnp.where(first, zero, rows)
        else:
            send_ref[i - 1] = jnp.where(first, out[:, half:], out[:, :half])


def project_kernel(place, g_ref, p_ref, _, own_ref, send_ref):
    half = p_ref.shape[2]
    first = place[0] == 0
    grads = split(g_ref[...])
    for i in range(own_ref.shape[0]):
        weights = jnp.concatenate([p_ref[:, 2 * i, :], p_ref[:, 2 * i + 1, :]], axis=1)
        out = product(grads, split(weights), NN)
        own_ref[i] = jnp.where(first, out[:, :half], out[:, half:])
        send_ref[i] = jnp.where(first, out[:, half:], out[:, :half])


def chain_kernel(place, r0, r1, r2, r3, u0, u1, u2, u3, high_ref, low_ref, query_ref,
                 fh, fl, dh, dl, rs):
    solved = rs.shape[0]
    panel = rs.shape[2]
    x, z, ex = place[0], place[1], place[2]
    piece = u0.shape[1]
    half = panel // 2
    ex_rows = rs.shape[1] - query_ref.shape[0]
    for d, ref in enumerate((r0, r1, r2, r3)):
        rs[lax.rem(z + solved - d, solved)] = ref[...]
    lower = solved - 1
    each = lower + solved
    for flip, ref in ((0, u0), (2, u1), (1, u2), (3, u3)):
        source = ex ^ flip
        for xi in range(2):
            row = pl.multiple_of((x ^ xi) * half + source * piece, piece)
            for b in range(lower):
                high, low = split(ref[each * xi + b])
                fh[z * lower + b, pl.ds(row, piece), :] = high
                fl[z * lower + b, pl.ds(row, piece), :] = low
            for j in range(solved):
                high, low = split(ref[each * xi + lower + j])
                dh[j, pl.ds(row, piece), :] = high
                dl[j, pl.ds(row, piece), :] = low
            for d in range(1, solved):
                owner = lax.rem(z + solved - d, solved)
                for b in range(lower):
                    high, low = split(ref[2 * each + 2 * lower * (d - 1) + lower * xi + b])
                    fh[owner * lower + b, pl.ds(row, piece), :] = high
                    fl[owner * lower + b, pl.ds(row, piece), :] = low
    for j in range(solved):
        out = product(split(rs[j]), (dh[j], dl[j]), NN)
        high, low = split(out)
        high_ref[:, j * panel:(j + 1) * panel] = high
        low_ref[:, j * panel:(j + 1) * panel] = low
        query_ref[:, j * panel:(j + 1) * panel] = out[ex_rows:, :]
        for i in range(j + 1, solved):
            rs[i] -= product((high, low), (fh[i * lower + j], fl[i * lower + j]), NT)


def update_kernel(place, wh, wl, f_ref, own_ref, q_ref, pre_ref, tq_ref):
    half = own_ref.shape[2]
    ex_rows = own_ref.shape[1]
    panel = f_ref.shape[1] // pl.num_programs(0) * 0 + 2 * half
    rows = f_ref[...]
    row = lax.broadcasted_iota(jnp.int32, rows.shape, 0)
    column = lax.broadcasted_iota(jnp.int32, rows.shape, 1)
    cut = (pl.program_id(0) == 0) & (row < half) & (column >= place[1] * panel)
    rows = jnp.where(cut, 0.0, rows)
    out = product((wh[...], wl[...]), split(rows), NT)
    for i in range(2):
        part = out[:, i * half:(i + 1) * half]
        pre_ref[i] = own_ref[i] - part[:ex_rows]
        tq_ref[i] = q_ref[i] - part[ex_rows:]


def finish_first_kernel(place, pre_ref, part_ref, recv_ref, _, out_ref):
    half = pre_ref.shape[2]
    ex_rows = pre_ref.shape[1]
    for i in range(pre_ref.shape[0]):
        if i == 0:
            other = jnp.where(place[0] == 0, part_ref[:ex_rows, :half], part_ref[:ex_rows, half:])
        else:
            other = recv_ref[i - 1]
        out_ref[i] = jnp.transpose(pre_ref[i] + other)


def finish_kernel(pre_ref, recv_ref, _, out_ref):
    for i in range(pre_ref.shape[0]):
        out_ref[i] = jnp.transpose(pre_ref[i] + recv_ref[i])


def score_kernel(place, scale, v_ref, c_ref, wh, wl, out_ref):
    mine = v_ref[...]
    other = c_ref[...]
    even = place[3] == 0
    both = jnp.concatenate([jnp.where(even, mine, other), jnp.where(even, other, mine)], axis=0)
    out_ref[...] = product(split(both), (wh[...], wl[...]), NT) / scale


def fast_device(gradients, projection, factor, diag_inverse, queries):
    rounds, panel = projection.shape[1], projection.shape[3]
    depth = projection.shape[0]
    half = factor.shape[2]
    width = factor.shape[3]
    ex_rows = gradients.shape[0]
    q_rows = queries.shape[3]
    columns = ex_rows + q_rows
    solved = diag_inverse.shape[0]
    feat = lax.axis_size("feat")
    ex_count = lax.axis_size("ex")
    x, z, ex = lax.axis_index("param"), lax.axis_index("feat"), lax.axis_index("ex")
    place = jnp.stack([x, z, ex, ex % 2]).astype(jnp.int32)
    tile = 4
    tiles = rounds // tile
    f32 = jnp.float32

    def across(value):
        return lax.ppermute(value, "param", [(0, 1), (1, 0)])

    def flip(value, bit):
        return lax.ppermute(value, "ex", [(i, i ^ bit) for i in range(ex_count)])

    def shift(value, by):
        return lax.ppermute(value, "feat", [(i, (i + by) % feat) for i in range(feat)])

    q_t = jnp.transpose(queries[:, 0], (0, 2, 1))
    p_t = projection.reshape(depth, rounds * 2, half)
    f_t = factor.reshape(rounds * half, width)

    piece = half // ex_count
    f_piece = lax.dynamic_slice(f_t, (ex * piece, 0), (piece, (solved - 1) * panel))
    f_piece = jnp.transpose(f_piece.reshape(piece, solved - 1, panel), (1, 0, 2))
    d_piece = lax.dynamic_slice(diag_inverse, (0, ex * piece, 0), (solved, piece, panel))
    piece_own = jnp.concatenate([f_piece, d_piece], axis=0)
    piece_other = across(piece_own)
    along = jnp.concatenate([piece_own[: solved - 1], piece_other[: solved - 1]], axis=0)
    along_got = [shift(along, d) for d in range(1, feat)]
    bundle = jnp.concatenate([piece_own, piece_other] + along_got, axis=0)
    bundle_y = flip(bundle, 2)
    bundle_c = flip(bundle, 1)
    bundle_yc = flip(bundle_y, 1)

    own_shape = jax.ShapeDtypeStruct((rounds, ex_rows, half), f32)
    own_spec = lambda t: pl.BlockSpec((tile, ex_rows, half), lambda i, t=t: (t, 0, 0))
    full = lambda shape: pl.BlockSpec(shape, lambda i: (0,) * len(shape))
    p_spec = lambda t: pl.BlockSpec((depth, 2 * tile, half), lambda i, t=t: (0, t, 0))
    own, send0, part = pl.pallas_call(
        project_first_kernel,
        grid=(1,),
        in_specs=[SMEM_SPEC, full((ex_rows, depth)), p_spec(0), full((1, q_rows, half))],
        out_specs=[own_spec(0), full((tile - 1, ex_rows, half)), full((columns, panel))],
        out_shape=[
            own_shape,
            jax.ShapeDtypeStruct((tile - 1, ex_rows, half), f32),
            jax.ShapeDtypeStruct((columns, panel), f32),
        ],
        name="project_first",
    )(place, gradients, p_t, q_t)
    sends = [send0]
    part_other = across(part)
    recvs = [across(send0)]
    for t in range(1, tiles):
        own, send = pl.pallas_call(
            project_kernel,
            grid=(1,),
            in_specs=[SMEM_SPEC, full((ex_rows, depth)), p_spec(t), ANY_SPEC],
            out_specs=[own_spec(t), full((tile, ex_rows, half))],
            out_shape=[own_shape, jax.ShapeDtypeStruct((tile, ex_rows, half), f32)],
            input_output_aliases={3: 0},
            name="project",
        )(place, gradients, p_t, own)
        sends.append(send)
        recvs.append(across(send))

    rows = part + part_other
    rows_got = [shift(rows, d) for d in range(1, feat)]
    high, low, window_q = pl.pallas_call(
        chain_kernel,
        grid=(1,),
        in_specs=[SMEM_SPEC] + [full((columns, panel))] * feat + [full(bundle.shape)] * ex_count,
        out_specs=[full((columns, width)), full((columns, width)), full((q_rows, width))],
        out_shape=[
            jax.ShapeDtypeStruct((columns, width), jnp.bfloat16),
            jax.ShapeDtypeStruct((columns, width), jnp.bfloat16),
            jax.ShapeDtypeStruct((q_rows, width), f32),
        ],
        scratch_shapes=[
            pltpu.VMEM((feat * (solved - 1), panel, panel), jnp.bfloat16),
            pltpu.VMEM((feat * (solved - 1), panel, panel), jnp.bfloat16),
            pltpu.VMEM((solved, panel, panel), jnp.bfloat16),
            pltpu.VMEM((solved, panel, panel), jnp.bfloat16),
            pltpu.VMEM((solved, columns, panel), f32),
        ],
        name="chain",
    )(place, rows, *rows_got, bundle, bundle_y, bundle_c, bundle_yc)

    window_y = flip(window_q, 2)
    wanted = jnp.where(ex // 2 == x, window_q, window_y)
    wanted_c = flip(wanted, 1)
    scores = pl.pallas_call(
        functools.partial(score_kernel, scale=math.sqrt(width)) if False else
        (lambda place, v, c, h, l, o: score_kernel(place, math.sqrt(width), v, c, h, l, o)),
        grid=(1,),
        in_specs=[SMEM_SPEC, full((q_rows, width)), full((q_rows, width)),
                  full((ex_rows, width)), full((ex_rows, width))],
        out_specs=full((2 * q_rows, ex_rows)),
        out_shape=jax.ShapeDtypeStruct((2 * q_rows, ex_rows), f32),
        name="scores",
    )(place, wanted, wanted_c, high, low)

    pre, tq = pl.pallas_call(
        update_kernel,
        grid=(rounds // 2,),
        in_specs=[
            SMEM_SPEC,
            full((columns, width)),
            full((columns, width)),
            pl.BlockSpec((2 * half, width), lambda i: (i, 0)),
            pl.BlockSpec((2, ex_rows, half), lambda i: (i, 0, 0)),
            pl.BlockSpec((2, q_rows, half), lambda i: (i, 0, 0)),
        ],
        out_specs=[
            pl.BlockSpec((2, ex_rows, half), lambda i: (i, 0, 0)),
            pl.BlockSpec((2, q_rows, half), lambda i: (i, 0, 0)),
        ],
        out_shape=[own_shape, jax.ShapeDtypeStruct((rounds, q_rows, half), f32)],
        name="update",
    )(place, high, low, f_t, own, q_t)

    out_shape = jax.ShapeDtypeStruct((rounds, half, ex_rows), f32)
    one = lambda t: pl.BlockSpec((1, ex_rows, half), lambda i, t=t: (t * tile + i, 0, 0))
    trailing = None
    for t in range(tiles):
        out_spec = pl.BlockSpec((tile, half, ex_rows), lambda i, t=t: (t, 0, 0))
        if t == 0:
            trailing = pl.pallas_call(
                lambda place, a, b, c, o: finish_first_kernel(place, a, b, c, None, o),
                grid=(1,),
                in_specs=[SMEM_SPEC, own_spec(0), full((columns, panel)), full((tile - 1, ex_rows, half))],
                out_specs=out_spec,
                out_shape=out_shape,
                name="finish_first",
            )(place, pre, part_other, recvs[0])
        else:
            trailing = pl.pallas_call(
                finish_kernel,
                grid=(tile,),
                in_specs=[one(t), pl.BlockSpec((1, ex_rows, half), lambda i: (i, 0, 0)), ANY_SPEC],
                out_specs=pl.BlockSpec((1, half, ex_rows), lambda i, t=t: (t * tile + i, 0, 0)),
                out_shape=out_shape,
                input_output_aliases={2: 0},
                name="finish",
            )(pre, recvs[t], trailing)
    trailing_queries = jnp.transpose(tq, (0, 2, 1))[:, None]
    return (scores, trailing[:, None], trailing_queries)


def fits(mesh_shape, gradients, projection, factor, diag_inverse, queries):
    half = factor.shape[2]
    solved = diag_inverse.shape[0]
    return (
        mesh_shape["param"] == 2
        and mesh_shape["ex"] == 4
        and mesh_shape["feat"] == solved == 4
        and half % 128 == 0
        and projection.shape[3] == 2 * half
        and factor.shape[3] == solved * 2 * half
        and projection.shape[1] % 4 == 0
        and gradients.shape[0] % 128 == 0
        and gradients.shape[1] % 128 == 0
        and queries.shape[3] % 16 == 0
    )


def solution(mesh):
    def per_device(*arrays):
        if fits(dict(mesh.shape), *arrays):
            return fast_device(*arrays)
        return plain_device(*arrays)

    return jax.shard_map(
        per_device,
        mesh=mesh,
        in_specs=(
            P("ex", "param"),
            P("param", None, "feat", None),
            P(None, "feat", "param", None),
            P(None, "param", None),
            P(None, "feat", "param", "ex"),
        ),
        out_specs=(
            P("param", "ex"),
            P(None, "feat", "param", "ex"),
            P(None, "feat", "param", "ex"),
        ),
        check_vma=False,
    )
```
